512 devices in a mesh: src: 4 (over z_lo), shard: 16 (over y, core), slab: 8 (over z_hi, x).
Axes of the slice: x: 4, y: 8, z: 8 (z_hi: 2, z_lo: 4; z = z_hi * 4 + z_lo), core: 2. Of those that a mesh axis runs over, the one named last changes fastest.
Arguments:
- src_feat: bfloat16 [4, 256, 256, 256], P('src', 'slab', 'shard'), may hold values from -6 to 6
- coords: int32 [4, 2], P('src'), may hold values from 0 to 6
- offsets: int32 [8], P('slab'), may hold values from 0 to 2128
- weights: bfloat16 [4, 2, 9, 512, 128], P('src'), may hold values from -0.09375 to 0.09375
Outputs:
- target_feat: bfloat16 [4, 256, 256, 256], P('src', 'slab', 'shard')
The draws below stay inside these ranges and needn't reach their ends.
All inputs are finite; a program needn't handle non-finite values.
Results may differ from the reference program's by a relative error of at most 0.0047.
Values may be sent and summed in bfloat16 or wider, within the bound.
A program may use at most 64 MiB of HBM per device.

```python
import math
import jax
import jax.numpy as jnp
from jax import lax

VIEWS = 4
C = 256
GROUPS = 2
ROWS = 32
IMAGE_H = 2160
SLABS = 8
H = 256
W = 256
TARGETS = 4


def touch_ends(array, stream_key, low, high):
    longest = array.shape.index(max(array.shape))
    spots = []
    for shift in (0, 1):
        where = [jax.random.randint(jax.random.fold_in(stream_key, axis), (), 0, length) for axis, length in enumerate(array.shape)]
        where[longest] = (where[longest] + shift) % array.shape[longest]
        spots.append(tuple(where))
    return array.at[spots[0]].set(low).at[spots[1]].set(high)


def steps_of(key, extent, shards, low, top_value):
    def one(dim, blocks):
        draws = jax.random.uniform(jax.random.fold_in(jax.random.fold_in(key, 6), dim), (blocks,), jnp.float32, low / len(shards), top_value / len(shards))
        return jnp.repeat(jnp.exp(draws), extent[dim] // blocks).reshape((-1,) + (1,) * (len(extent) - dim - 1))

    gain = one(*shards[0])
    for cut in shards[1:]:
        gain = gain * one(*cut)
    return gain


def noise(rng, shape, spread, bound, shards=(), kind=jnp.bfloat16):
    entries = spread * jax.random.normal(rng, shape, jnp.float32)
    if shards:
        entries = entries * steps_of(rng, shape, shards, -0.22, 0.18)
    return jnp.clip(entries, -bound, bound).astype(kind)


def setup_inputs(seed: int = 0) -> dict:
    arg_keys = jax.random.split(jax.random.key(seed), 5)
    src_feat = noise(arg_keys[0], (VIEWS, H, W, C), 1.0, 6.0, ((0, 4), (1, 8), (2, 16)))
    coords = touch_ends(jax.random.randint(arg_keys[1], (TARGETS, 2), 0, 7), jax.random.fold_in(arg_keys[1], 1), 0, 6).astype(jnp.int32)
    offsets = touch_ends(jax.random.randint(arg_keys[2], (SLABS,), 0, IMAGE_H - ROWS + 1), jax.random.fold_in(arg_keys[2], 1), 0, IMAGE_H - ROWS).astype(jnp.int32)
    weights = noise(arg_keys[3], (TARGETS, GROUPS, 9, VIEWS * C // GROUPS, C // GROUPS), (9 * VIEWS * C // GROUPS) ** -0.5, 0.09375, ((0, 4),))
    return dict(src_feat=src_feat, coords=coords, offsets=offsets, weights=weights)


def encoding(rowpos, chan_count):
    channel_idx = jnp.arange(chan_count, dtype=jnp.int32)
    halves = (channel_idx // 2).astype(jnp.float32)
    frequency = jnp.exp(-math.log(1000.0) * halves / (chan_count / 2))
    phases = (channel_idx % 2).astype(jnp.float32) * (math.pi / 2)
    return jnp.sin(rowpos.astype(jnp.float32)[:, None] * frequency[None, :] + phases[None, :])


def blend_weights(coords):
    vertical = coords[:, 0].astype(jnp.float32) / 6.0
    across = coords[:, 1].astype(jnp.float32) / 6.0
    return jnp.stack([(1.0 - vertical) * (1.0 - across), (1.0 - vertical) * across,
                      vertical * (1.0 - across), vertical * across], axis=1)


def reference(src_feat, coords, offsets, weights):
    rowpos = (offsets[:, None] + jnp.arange(ROWS, dtype=jnp.int32)[None, :]).reshape(-1)
    encoded = encoding(rowpos, C)
    posed = (src_feat.astype(jnp.float32) + encoded[None, :, None, :]).astype(jnp.bfloat16)
    padded = jnp.pad(posed, ((0, 0), (1, 1), (1, 1), (0, 0)))
    height = posed.shape[1]
    img_width = posed.shape[2]
    per_group = VIEWS // GROUPS
    grouped = padded.reshape(GROUPS, per_group, height + 2, img_width + 2, C)
    grouped = grouped.transpose(0, 2, 3, 1, 4).reshape(GROUPS, height + 2, img_width + 2, per_group * C)
    mixing = blend_weights(coords)
    posed_wide = posed.astype(jnp.float32)

    def one_target(packed):
        kernel, mixture = packed
        group_parts = []
        for group_idx in range(GROUPS):
            running = jnp.zeros((height * img_width, C // GROUPS), jnp.float32)
            for tap_index in range(9):
                tap_row = tap_index // 3
                tap_col = tap_index % 3
                window = grouped[group_idx, tap_row:tap_row + height, tap_col:tap_col + img_width, :]
                window = window.reshape(height * img_width, per_group * C)
                running = running + jnp.dot(window, kernel[group_idx, tap_index], preferred_element_type=jnp.float32)
            group_parts.append(running.reshape(height, img_width, C // GROUPS))
        convolved = jnp.concatenate(group_parts, axis=-1)
        blended = jnp.einsum("v,vhwc->hwc", mixture, posed_wide)
        return (blended + jax.nn.silu(convolved)).astype(jnp.bfloat16)

    return lax.map(one_target, (weights, mixing))
```

```python
import functools
import math

import jax
import jax.numpy as jnp
from jax import lax
from jax.experimental import pallas as pl
from jax.experimental.pallas import tpu as pltpu
from jax.sharding import PartitionSpec as P

VIEWS = 4
CHUNKS = 4
EDGE = 8
MESH = pl.DeviceIdType.MESH


def encoding(offset, first_row, row_count, chans):
    row_idx = lax.broadcasted_iota(jnp.int32, (row_count, chans), 0)
    rowpos = (offset + first_row + row_idx).astype(jnp.float32)
    chan = lax.broadcasted_iota(jnp.int32, (row_count, chans), 1)
    halves = (chan // 2).astype(jnp.float32)
    frequency = jnp.exp(-math.log(1000.0) * halves / (chans / 2))
    phases = (chan % 2).astype(jnp.float32) * (math.pi / 2)
    return jnp.sin(rowpos * frequency + phases)


def kernel(sizes, coords_ref, offsets_ref, src_hbm, w_ref, out_ref, src_ref, panel, weights, acc_side, acc_mid,
           src_sem, w_sem, z_send, z_recv, col_send, col_recv, row_send, row_recv):
    shards, slabs = sizes
    rows, cols, chans = src_ref.shape
    groups, _, depth, width = w_ref.shape
    chunk_rows = rows // CHUNKS
    s, h, b = lax.axis_index("src"), lax.axis_index("shard"), lax.axis_index("slab")
    below, above = s > 0, s < VIEWS - 1
    has_left, has_right = h > 0, h < shards - 1
    has_top, has_bottom = b > 0, b < slabs - 1
    partners = (
        (below, {"src": s - 1}), (above, {"src": s + 1}),
        (has_left, {"shard": h - 1}), (has_right, {"shard": h + 1}),
        (has_top, {"slab": b - 1}), (has_bottom, {"slab": b + 1}),
    )

    src_copy = pltpu.make_async_copy(src_hbm, src_ref, src_sem)
    src_copy.start()
    barrier = pltpu.get_barrier_semaphore()
    for present, target in partners:
        @pl.when(present)
        def _():
            pl.semaphore_signal(barrier, inc=1, device_id=target, device_id_type=MESH)

    def weight_copy(i):
        g, tap = i // 9, i % 9
        a, c = tap // 3, tap % 3
        lane = (0, 2, 1)[c] * width
        return pltpu.make_async_copy(
            w_ref.at[g, tap], weights.at[g, a, :, lane:lane + width], w_sem.at[i])

    for i in range(groups * 9):
        weight_copy(i).start()

    acc_side[...] = jnp.zeros_like(acc_side)
    acc_mid[...] = jnp.zeros_like(acc_mid)

    @pl.when(jnp.logical_not(has_left))
    def _():
        panel[:, 1:rows + 1, cols:cols + EDGE, :] = jnp.zeros((VIEWS, rows, EDGE, chans), panel.dtype)

    @pl.when(jnp.logical_not(has_right))
    def _():
        panel[:, 1:rows + 1, cols + EDGE:, :] = jnp.zeros((VIEWS, rows, EDGE, chans), panel.dtype)

    @pl.when(jnp.logical_not(has_top))
    def _():
        panel[:, 0] = jnp.zeros((VIEWS, cols + 2 * EDGE, chans), panel.dtype)

    @pl.when(jnp.logical_not(has_bottom))
    def _():
        panel[:, rows + 1] = jnp.zeros((VIEWS, cols + 2 * EDGE, chans), panel.dtype)

    src_copy.wait()
    pl.semaphore_wait(barrier, sum(present.astype(jnp.int32) for present, _ in partners))

    def chunk_start(k):
        return ((CHUNKS - 1) * k) % CHUNKS * chunk_rows

    def z_copy(v, k, up):
        part = panel.at[v, pl.ds(1 + chunk_start(k), chunk_rows), 0:cols, :]
        return pltpu.make_async_remote_copy(
            src_ref=part, dst_ref=part, send_sem=z_send.at[up, v, k], recv_sem=z_recv.at[v, k],
            device_id={"src": s + 1 if up else s - 1}, device_id_type=MESH)

    def col_copy(v, k, right):
        at = pl.ds(1 + chunk_start(k), chunk_rows)
        src = panel.at[v, at, cols - EDGE:cols, :] if right else panel.at[v, at, 0:EDGE, :]
        dst = panel.at[v, at, cols:cols + EDGE, :] if right else panel.at[v, at, cols + EDGE:, :]
        return pltpu.make_async_remote_copy(
            src_ref=src, dst_ref=dst, send_sem=col_send.at[right, v, k], recv_sem=col_recv.at[right, v, k],
            device_id={"shard": h + 1 if right else h - 1}, device_id_type=MESH)

    def row_copy(v, down):
        return pltpu.make_async_remote_copy(
            src_ref=panel.at[v, rows if down else 1], dst_ref=panel.at[v, 0 if down else rows + 1],
            send_sem=row_send.at[down, v], recv_sem=row_recv.at[down, v],
            device_id={"slab": b + 1 if down else b - 1}, device_id_type=MESH)

    def arrive(v, k, up, own):
        if own:
            start = chunk_start(k)
            encoded = encoding(offsets_ref[0], start, chunk_rows, chans)
            feat = src_ref[pl.ds(start, chunk_rows)].astype(jnp.float32)
            panel[v, pl.ds(1 + start, chunk_rows), 0:cols, :] = (feat + encoded[:, None, :]).astype(panel.dtype)
        else:
            z_copy(v, k, up).wait_recv()
        for direction, present in ((1, above), (0, below)):
            if own or direction == up:
                @pl.when(present)
                def _():
                    z_copy(v, k, direction).start()
        for right, present in ((1, has_right), (0, has_left)):
            @pl.when(present)
            def _():
                col_copy(v, k, right).start()

    def border(v, k):
        for right, present in ((1, has_left), (0, has_right)):
            @pl.when(present)
            def _():
                col_copy(v, k, right).wait_recv()

        @pl.when((k == 0) & has_top)
        def _():
            row_copy(v, 0).start()

        @pl.when((k == 1) & has_bottom)
        def _():
            row_copy(v, 1).start()

    def multiply(v, k):
        @pl.when(k == 0)
        def _():
            for down, present in ((1, has_top), (0, has_bottom)):
                @pl.when(present)
                def _():
                    row_copy(v, down).wait_recv()

        @pl.when(k < 3)
        def _():
            g = v // 2
            taken = pl.ds(pl.multiple_of((v % 2) * chans, chans), chans)
            full = panel[v, pl.ds(k, rows), :, :].reshape(rows * (cols + 2 * EDGE), chans)
            acc_side[g] += jnp.dot(full, weights[g, k, taken, 0:2 * width], preferred_element_type=jnp.float32)
            own = panel[v, pl.ds(k, rows), 0:cols, :].reshape(rows * cols, chans)
            acc_mid[g] += jnp.dot(own, weights[g, k, taken, 2 * width:], preferred_element_type=jnp.float32)

    def for_views(item, act, live):
        d, k = item // CHUNKS, item % CHUNKS

        @pl.when(live & (d == 0))
        def _():
            act(s, k, 1, True)

        @pl.when(live & (d > 0) & (s - d >= 0))
        def _():
            act(s - d, k, 1, False)

        @pl.when(live & (d > 0) & (s + d < VIEWS))
        def _():
            act(s + d, k, 0, False)

    items = VIEWS * CHUNKS
    lag = CHUNKS + 1

    @pl.loop(0, items + lag)
    def _(i):
        @pl.when(i == lag)
        def _():
            for n in range(groups * 9):
                weight_copy(n).wait()

        for_views(i, arrive, i < items)
        for_views(i - 1, lambda v, k, up, own: border(v, k), (i >= 1) & (i - 1 < items))
        for_views(i - lag, lambda v, k, up, own: multiply(v, k), i >= lag)

    vertical = coords_ref[0, 0].astype(jnp.float32) / 6.0
    across = coords_ref[0, 1].astype(jnp.float32) / 6.0
    mixing = ((1.0 - vertical) * (1.0 - across), (1.0 - vertical) * across,
              vertical * (1.0 - across), vertical * across)

    @pl.loop(0, rows // EDGE)
    def _(i):
        at = pl.ds(i * EDGE, EDGE)
        for g in range(groups):
            lanes = slice(g * width, (g + 1) * width)
            side = acc_side[g, pl.ds(pl.multiple_of(i * EDGE * (cols + 2 * EDGE), EDGE), EDGE * (cols + 2 * EDGE)), :]
            side = side.reshape(EDGE, cols + 2 * EDGE, 2 * width)
            joined = acc_mid[g, pl.ds(pl.multiple_of(i * EDGE * cols, EDGE), EDGE * cols), :].reshape(EDGE, cols, width)
            joined += jnp.concatenate([side[:, cols + EDGE - 1:cols + EDGE, :width], side[:, 0:cols - 1, :width]], axis=1)
            joined += jnp.concatenate([side[:, 1:cols, width:], side[:, cols + EDGE:cols + EDGE + 1, width:]], axis=1)
            blended = jnp.zeros((EDGE, cols, width), jnp.float32)
            for v in range(VIEWS):
                blended += mixing[v] * panel[v, pl.ds(1 + i * EDGE, EDGE), 0:cols, lanes].astype(jnp.float32)
            out_ref[at, :, lanes] = (blended + joined / (1.0 + jnp.exp(-joined))).astype(out_ref.dtype)

    for k in range(CHUNKS):
        for v in range(VIEWS):
            @pl.when(above & (s >= v))
            def _():
                z_copy(v, k, 1).wait_send()

            @pl.when(below & (s <= v))
            def _():
                z_copy(v, k, 0).wait_send()

            for right, present in ((1, has_right), (0, has_left)):
                @pl.when(present)
                def _():
                    col_copy(v, k, right).wait_send()
    for v in range(VIEWS):
        for down, present in ((1, has_bottom), (0, has_top)):
            @pl.when(present)
            def _():
                row_copy(v, down).wait_send()


def local(sizes, src_feat, coords, offsets, weights):
    _, rows, cols, chans = src_feat.shape
    _, groups, taps, depth, width = weights.shape
    wide = cols + 2 * EDGE
    dma = pltpu.SemaphoreType.DMA
    out = pl.pallas_call(
        functools.partial(kernel, sizes),
        out_shape=jax.ShapeDtypeStruct((rows, cols, chans), jnp.bfloat16),
        in_specs=[
            pl.BlockSpec(memory_space=pltpu.SMEM),
            pl.BlockSpec(memory_space=pltpu.SMEM),
            pl.BlockSpec(memory_space=pltpu.HBM),
            pl.BlockSpec(memory_space=pltpu.HBM),
        ],
        out_specs=pl.BlockSpec(memory_space=pltpu.VMEM),
        scratch_shapes=[
            pltpu.VMEM((rows, cols, chans), jnp.bfloat16),
            pltpu.VMEM((VIEWS, rows + 2, wide, chans), jnp.bfloat16),
            pltpu.VMEM((groups, 3, depth, 3 * width), jnp.bfloat16),
            pltpu.VMEM((groups, rows * wide, 2 * width), jnp.float32),
            pltpu.VMEM((groups, rows * cols, width), jnp.float32),
            dma,
            dma((groups * taps,)),
            dma((2, VIEWS, CHUNKS)),
            dma((VIEWS, CHUNKS)),
            dma((2, VIEWS, CHUNKS)),
            dma((2, VIEWS, CHUNKS)),
            dma((2, VIEWS)),
            dma((2, VIEWS)),
        ],
        compiler_params=pltpu.CompilerParams(
            collective_id=0, has_side_effects=True, vmem_limit_bytes=40 << 20),
    )(coords, offsets, src_feat[0], weights[0])
    return out[None]


def solution(mesh):
    sizes = (mesh.shape["shard"], mesh.shape["slab"])
    in_specs = (
        P("src", "slab", "shard", None),
        P("src", None),
        P("slab"),
        P("src", None, None, None, None),
    )
    out_specs = P("src", "slab", "shard", None)
    return jax.shard_map(functools.partial(local, sizes), mesh=mesh, in_specs=in_specs, out_specs=out_specs,
                         check_vma=False)
```

```python
import functools
import math

import jax
import jax.numpy as jnp
from jax import lax
from jax.experimental import pallas as pl
from jax.experimental.pallas import tpu as pltpu
from jax.sharding import PartitionSpec as P

VIEWS = 4
CHUNKS = 4
EDGE = 8
MESH = pl.DeviceIdType.MESH


def encoding(offset, first_row, row_count, chans):
    row_idx = lax.broadcasted_iota(jnp.int32, (row_count, chans), 0)
    rowpos = (offset + first_row + row_idx).astype(jnp.float32)
    chan = lax.broadcasted_iota(jnp.int32, (row_count, chans), 1)
    halves = (chan // 2).astype(jnp.float32)
    frequency = jnp.exp(-math.log(1000.0) * halves / (chans / 2))
    phases = (chan % 2).astype(jnp.float32) * (math.pi / 2)
    return jnp.sin(rowpos * frequency + phases)


def count(*conditions):
    return sum(condition.astype(jnp.int32) for condition in conditions)


def kernel(sizes, coords_ref, offsets_ref, src_hbm, w_hbm, out_hbm, src, panel, halo, weights, side_acc, mid_acc,
           blend, out, src_sem, w_sem, out_sem, z_send, z_recv, col_send, col_recv, row_send, row_recv, cross_send,
           z_ready, col_ready, row_ready, cross_ready):
    shards, slabs = sizes
    rows, cols, chans = src.shape
    groups, _, depth, width = w_hbm.shape[0], None, w_hbm.shape[2], w_hbm.shape[3]
    wide = cols + 2 * EDGE
    step_rows = rows // CHUNKS
    s, h, b = lax.axis_index("src"), lax.axis_index("shard"), lax.axis_index("slab")
    below, above = s > 0, s < VIEWS - 1
    has_left, has_right = h > 0, h < shards - 1
    has_top, has_bottom = b > 0, b < slabs - 1
    cross_bottom, cross_top = b == slabs // 2 - 1, b == slabs // 2
    near_top, near_bottom = has_top & jnp.logical_not(cross_top), has_bottom & jnp.logical_not(cross_bottom)

    def signal(sem, target):
        pl.semaphore_signal(sem, inc=1, device_id=target, device_id_type=MESH)

    src_copy = pltpu.make_async_copy(src_hbm, src, src_sem)
    src_copy.start()

    barrier = pltpu.get_barrier_semaphore()
    for present, targets in (
        (below, ({"src": s - 1},)),
        (has_left, ({"shard": h - 1},)),
        (near_top, ({"slab": b - 1},)),
        (cross_bottom, tuple({"src": t, "slab": b + 1} for t in range(VIEWS))),
    ):
        @pl.when(present)
        def _():
            for target in targets:
                signal(barrier, target)
    expected = count(above, has_right, near_bottom) + VIEWS * count(cross_top)

    @pl.when(expected > 0)
    def _():
        pl.semaphore_wait(barrier, expected)

    for present, sem, targets in (
        (above, z_ready, ({"src": s + 1},)),
        (has_right, col_ready, ({"shard": h + 1},)),
        (near_bottom, row_ready, ({"slab": b + 1},)),
        (cross_top, cross_ready, tuple({"src": t, "slab": b - 1} for t in range(VIEWS))),
    ):
        @pl.when(present)
        def _():
            for target in targets:
                signal(sem, target)

    def weight_copy(i):
        g, tap = i // 9, i % 9
        lane = (0, 2, 1)[tap % 3] * width
        return pltpu.make_async_copy(
            w_hbm.at[g, tap], weights.at[g, tap // 3, :, lane:lane + width], w_sem.at[i])

    def chunk_start(k):
        return ((CHUNKS - 1) * k) % CHUNKS * step_rows

    def z_copy(v, k, up):
        part = panel.at[v, pl.ds(chunk_start(k), step_rows), 0:cols, :]
        return pltpu.make_async_remote_copy(
            src_ref=part, dst_ref=part, send_sem=z_send.at[up, v, k], recv_sem=z_recv.at[v, k],
            device_id={"src": s + 1 if up else s - 1}, device_id_type=MESH)

    def col_copy(v, k, right):
        at = pl.ds(chunk_start(k), step_rows)
        part = panel.at[v, at, cols - EDGE:cols, :] if right else panel.at[v, at, 0:EDGE, :]
        into = panel.at[v, at, cols:cols + EDGE, :] if right else panel.at[v, at, cols + EDGE:, :]
        return pltpu.make_async_remote_copy(
            src_ref=part, dst_ref=into, send_sem=col_send.at[right, v, k], recv_sem=col_recv.at[right, v, k],
            device_id={"shard": h + 1 if right else h - 1}, device_id_type=MESH)

    def row_copy(v, down):
        return pltpu.make_async_remote_copy(
            src_ref=panel.at[v, rows - 1 if down else 0], dst_ref=halo.at[1 - down, v],
            send_sem=row_send.at[down, v], recv_sem=row_recv.at[down, v],
            device_id={"slab": b + 1 if down else b - 1}, device_id_type=MESH)

    def cross_copy(t, down):
        return pltpu.make_async_remote_copy(
            src_ref=panel.at[s, rows - 1 if down else 0], dst_ref=halo.at[1 - down, s],
            send_sem=cross_send.at[t], recv_sem=row_recv.at[down, s],
            device_id={"src": t, "slab": b + 1 if down else b - 1}, device_id_type=MESH)

    vertical = coords_ref[0, 0].astype(jnp.float32) / 6.0
    across = coords_ref[0, 1].astype(jnp.float32) / 6.0

    def multiply(v, k):
        for right, present in ((1, has_left), (0, has_right)):
            @pl.when(present)
            def _():
                col_copy(v, k, right).wait_recv()

        g = v // 2
        start = chunk_start(k)
        at = pl.ds(start, step_rows)
        taken = pl.ds(pl.multiple_of((v % 2) * chans, chans), chans)
        full = panel[v, at, :, :].reshape(step_rows * wide, chans)
        own = panel[v, at, 0:cols, :]
        flat = own.reshape(step_rows * cols, chans)
        for a in range(3):
            side_at = pl.ds(pl.multiple_of((start + 2 - a) * wide, wide), step_rows * wide)
            side_acc[g, side_at, :] += jnp.dot(
                full, weights[g, a, taken, 0:2 * width], preferred_element_type=jnp.float32)
            mid_at = pl.ds(pl.multiple_of((start + 2 - a) * cols, cols), step_rows * cols)
            mid_acc[g, mid_at, :] += jnp.dot(
                flat, weights[g, a, taken, 2 * width:], preferred_element_type=jnp.float32)
        mix = jnp.where(v >= 2, vertical, 1.0 - vertical) * jnp.where(v % 2 == 1, across, 1.0 - across)
        blend[at] += mix * own.astype(jnp.float32)

    def send_rows(v):
        @pl.when(near_top)
        def _():
            row_copy(v, 0).start()

        @pl.when(near_bottom)
        def _():
            row_copy(v, 1).start()

    def multiply_rows(v):
        g = v // 2
        taken = pl.ds(pl.multiple_of((v % 2) * chans, chans), chans)
        for from_top, present, a, row in ((1, has_top, 0, 1), (0, has_bottom, 2, rows)):
            @pl.when(present)
            def _():
                row_copy(v, from_top).wait_recv()
                line = halo[1 - from_top, v]
                side_acc[g, row * wide:(row + 1) * wide, :] += jnp.dot(
                    line, weights[g, a, taken, 0:2 * width], preferred_element_type=jnp.float32)
                mid_acc[g, row * cols:(row + 1) * cols, :] += jnp.dot(
                    line[0:cols], weights[g, a, taken, 2 * width:], preferred_element_type=jnp.float32)

    def for_views(step, act):
        @pl.when(s - step >= 0)
        def _():
            act(s - step, 1)

        @pl.when((step > 0) & (s + step < VIEWS))
        def _():
            act(s + step, 0)

    src_copy.wait()

    @pl.loop(0, CHUNKS)
    def _(k):
        start = chunk_start(k)
        at = pl.ds(start, step_rows)
        encoded = encoding(offsets_ref[0], start, step_rows, chans)
        panel[s, at, 0:cols, :] = (src[at].astype(jnp.float32) + encoded[:, None, :]).astype(panel.dtype)

        @pl.when(above)
        def _():
            z_copy(s, k, 1).start()

        @pl.when(has_right)
        def _():
            col_copy(s, k, 1).start()

    @pl.when(below)
    def _():
        pl.semaphore_wait(z_ready, 1)

        @pl.loop(0, CHUNKS)
        def _(k):
            z_copy(s, k, 0).start()

    for i in range(groups * 9):
        weight_copy(i).start()

    @pl.when(has_left)
    def _():
        pl.semaphore_wait(col_ready, 1)

        @pl.loop(0, CHUNKS)
        def _(k):
            col_copy(s, k, 0).start()

    side_acc[...] = jnp.zeros_like(side_acc)
    mid_acc[...] = jnp.zeros_like(mid_acc)
    blend[...] = jnp.zeros_like(blend)

    @pl.when(jnp.logical_not(has_left))
    def _():
        panel[:, :, cols:cols + EDGE, :] = jnp.zeros((VIEWS, rows, EDGE, chans), panel.dtype)

    @pl.when(jnp.logical_not(has_right))
    def _():
        panel[:, :, cols + EDGE:, :] = jnp.zeros((VIEWS, rows, EDGE, chans), panel.dtype)

    for i in range(groups * 9):
        weight_copy(i).wait()

    @pl.loop(0, CHUNKS)
    def _(k):
        multiply(s, k)

        @pl.when((k == 0) & cross_top)
        def _():
            for t in range(VIEWS):
                cross_copy(t, 0).start()

    items = VIEWS * CHUNKS

    @pl.loop(CHUNKS, items + 1)
    def _(i):
        k = i % CHUNKS

        def arrive(v, up):
            z_copy(v, k, up).wait_recv()

            @pl.when(above if up else below)
            def _():
                z_copy(v, k, up).start()

            for right, present in ((1, has_right), (0, has_left)):
                @pl.when(present)
                def _():
                    col_copy(v, k, right).start()

        @pl.when(i < items)
        def _():
            for_views(i // CHUNKS, arrive)

        @pl.when(i == items)
        def _():
            for_views(VIEWS - 1, lambda v, up: multiply_rows(v))

        @pl.when(i > CHUNKS)
        def _():
            for_views((i - 1) // CHUNKS, lambda v, up: multiply(v, (i - 1) % CHUNKS))

        @pl.when(i == 2 * CHUNKS + 1)
        def _():
            @pl.when(near_top)
            def _():
                pl.semaphore_wait(row_ready, 1)

            @pl.when(cross_bottom)
            def _():
                pl.semaphore_wait(cross_ready, VIEWS)
                for t in range(VIEWS):
                    cross_copy(t, 1).start()

            for_views(0, lambda v, up: send_rows(v))
            for_views(1, lambda v, up: send_rows(v))

        @pl.when((i == 2 * CHUNKS + 2) | (i == 3 * CHUNKS + 2))
        def _():
            for_views(i // CHUNKS, lambda v, up: send_rows(v))

        @pl.when(i == 3 * CHUNKS + 2)
        def _():
            @pl.loop(0, VIEWS - 1)
            def _(step):
                for_views(step, lambda v, up: multiply_rows(v))

    def out_copy(j):
        at = pl.ds(j * EDGE, EDGE)
        return pltpu.make_async_copy(out.at[at], out_hbm.at[at], out_sem.at[j])

    @pl.loop(0, rows // EDGE)
    def _(j):
        at = pl.ds(j * EDGE, EDGE)
        for g in range(groups):
            lanes = slice(g * width, (g + 1) * width)
            side = side_acc[g, pl.ds(pl.multiple_of((j * EDGE + 1) * wide, wide), EDGE * wide), :]
            side = side.reshape(EDGE, wide, 2 * width)
            joined = mid_acc[g, pl.ds(pl.multiple_of((j * EDGE + 1) * cols, cols), EDGE * cols), :]
            joined = joined.reshape(EDGE, cols, width)
            joined += jnp.concatenate(
                [side[:, cols + EDGE - 1:cols + EDGE, :width], side[:, 0:cols - 1, :width]], axis=1)
            joined += jnp.concatenate(
                [side[:, 1:cols, width:], side[:, cols + EDGE:cols + EDGE + 1, width:]], axis=1)
            blended = blend[at, :, lanes]
            out[at, :, lanes] = (blended + joined / (1.0 + jnp.exp(-joined))).astype(out.dtype)
        out_copy(j).start()

    @pl.loop(0, CHUNKS)
    def _(k):
        out_copy(k).wait()
        for v in range(VIEWS):
            @pl.when(above & (s >= v))
            def _():
                z_copy(v, k, 1).wait_send()

            @pl.when(below & (s <= v))
            def _():
                z_copy(v, k, 0).wait_send()

            for right, present in ((1, has_right), (0, has_left)):
                @pl.when(present)
                def _():
                    col_copy(v, k, right).wait_send()

    @pl.loop(0, VIEWS)
    def _(v):
        for down, present in ((1, near_bottom), (0, near_top)):
            @pl.when(present)
            def _():
                row_copy(v, down).wait_send()

        for down, present in ((1, cross_bottom), (0, cross_top)):
            @pl.when(present)
            def _():
                cross_copy(v, down).wait_send()


def local(sizes, src_feat, coords, offsets, weights):
    _, rows, cols, chans = src_feat.shape
    _, groups, taps, depth, width = weights.shape
    wide = cols + 2 * EDGE
    dma, regular = pltpu.SemaphoreType.DMA, pltpu.SemaphoreType.REGULAR
    out = pl.pallas_call(
        functools.partial(kernel, sizes),
        out_shape=jax.ShapeDtypeStruct((rows, cols, chans), jnp.bfloat16),
        in_specs=[
            pl.BlockSpec(memory_space=pltpu.SMEM),
            pl.BlockSpec(memory_space=pltpu.SMEM),
            pl.BlockSpec(memory_space=pltpu.HBM),
            pl.BlockSpec(memory_space=pltpu.HBM),
        ],
        out_specs=pl.BlockSpec(memory_space=pltpu.HBM),
        scratch_shapes=[
            pltpu.VMEM((rows, cols, chans), jnp.bfloat16),
            pltpu.VMEM((VIEWS, rows, wide, chans), jnp.bfloat16),
            pltpu.VMEM((2, VIEWS, wide, chans), jnp.bfloat16),
            pltpu.VMEM((groups, 3, depth, 3 * width), jnp.bfloat16),
            pltpu.VMEM((groups, (rows + 2) * wide, 2 * width), jnp.float32),
            pltpu.VMEM((groups, (rows + 2) * cols, width), jnp.float32),
            pltpu.VMEM((rows, cols, chans), jnp.float32),
            pltpu.VMEM((rows, cols, chans), jnp.bfloat16),
            dma,
            dma((groups * taps,)),
            dma((CHUNKS,)),
            dma((2, VIEWS, CHUNKS)),
            dma((VIEWS, CHUNKS)),
            dma((2, VIEWS, CHUNKS)),
            dma((2, VIEWS, CHUNKS)),
            dma((2, VIEWS)),
            dma((2, VIEWS)),
            dma((VIEWS,)),
            regular,
            regular,
            regular,
            regular,
        ],
        compiler_params=pltpu.CompilerParams(
            collective_id=0, has_side_effects=True, vmem_limit_bytes=60 << 20),
    )(coords, offsets, src_feat[0], weights[0])
    return out[None]


def solution(mesh):
    sizes = (mesh.shape["shard"], mesh.shape["slab"])
    in_specs = (
        P("src", "slab", "shard", None),
        P("src", None),
        P("slab"),
        P("src", None, None, None, None),
    )
    out_specs = P("src", "slab", "shard", None)
    return jax.shard_map(functools.partial(local, sizes), mesh=mesh, in_specs=in_specs, out_specs=out_specs,
                         check_vma=False)
```
